32 devices in a mesh: swap: 2 (over core), ep: 16 (over z, y, x).
Axes of the slice: x: 2, y: 2, z: 4, core: 2. Of those that a mesh axis runs over, the one named last changes fastest.
Arguments:
- grad_out: bfloat16 [2048, 6144], P('ep'), may hold values from -6 to 6
- parked_inputs: bfloat16 [2, 2048, 3072], P('swap', 'ep'), may hold values from -6 to 6
- route_ids: int32 [2048, 2], P('ep'), may hold values from 0 to 7, all different within a row; in each aligned block of 128 rows (0 to 127, 128 to 255, ...) at most 34 rows name the same one
- route_probs: float32 [2048, 2], P('ep'), may hold values from 0.1 to 0.9
- flight_expert: int32 [1], replicated, may hold values from 0 to 7
- w_gate: bfloat16 [6144, 8192], P(None, 'ep'), may hold values from -0.078125 to 0.078125
- w_up: bfloat16 [6144, 8192], P(None, 'ep'), may hold values from -0.078125 to 0.078125
- w_down: bfloat16 [8192, 6144], P('ep'), may hold values from -0.0625 to 0.0625
Outputs:
- grad_in: bfloat16 [2048, 6144], P('ep', 'swap')
The draws below stay inside these ranges and needn't reach their ends.
Inputs may be any that keep to these rules, and one draw needn't show every extreme that they name: `route_ids`: each row names 2 different experts; the rows of one device name any one expert at most 34 times.
All inputs are finite; a program needn't handle non-finite values.
Results may differ from the reference program's by a relative error of at most 0.0024.
Values may be sent and summed in bfloat16 or wider, within the bound.
No kernel may reach another device: no remote copies, remote signals or barrier semaphores. Data moves between devices by JAX's collectives and lax.ppermute only.
A program may use at most 256 MiB of HBM per device.

```python
import math
import jax
import jax.numpy as jnp
import numpy as np
from jax import lax

D = 6144
EXPERTS = 8
TOPK = 2
FF = 8192
TOK = 128
CAP = 34
TOKENS = 2048
HALF = 3072
N_EP = 16


def steps_of(stream_key, shape, pieces, least, top_value):
    loudness = 1.0
    for axis_at, blocks in pieces:
        heights = jax.random.uniform(jax.random.fold_in(jax.random.fold_in(stream_key, 6), axis_at), (blocks,), jnp.float32, least / len(pieces), top_value / len(pieces))
        loudness = loudness * jnp.repeat(jnp.exp(heights), shape[axis_at] // blocks).reshape((-1,) + (1,) * (len(shape) - 1 - axis_at))
    return loudness


def shared_out(own_key, own, number, rows, number_of, top, bound, skew):
    ranking = jax.random.permutation(own_key, number_of)
    heavy_load, common = portions_of(number_of, rows * top, bound, skew, True), portions_of(number_of, rows * top, bound, skew, False)
    places = jnp.arange(number_of)

    def named(sizes, turn):
        used = int((sizes > 0).sum())
        fixed = max(1, used // 4)
        shifted = fixed + (places - fixed + turn * (used - fixed)) % max(1, number_of - fixed)
        return jnp.zeros((number_of,), jnp.int32).at[ranking[jnp.where(places < fixed, places, shifted)]].set(jnp.asarray(sizes, jnp.int32))

    sizes = jnp.where(number % 4 == 0, named(heavy_load, number // 4), named(common, number - number // 4 - 1))
    mixed = jax.random.permutation(jax.random.fold_in(own, 3), number_of)
    giver, taker = mixed[0:number_of // 2 * 2:2], mixed[1:number_of // 2 * 2:2]
    slack = jnp.minimum(sizes[giver] - 1, bound - sizes[taker]) // 2
    slack = jnp.where((giver == ranking[0]) | (taker == ranking[0]) | (sizes[taker] == 0), 0, jnp.maximum(slack, 0))
    shifted = jax.random.randint(jax.random.fold_in(own, 4), (number_of // 2,), 0, 1 << 20) % (slack + 1)
    sizes = sizes.at[giver].add(-shifted).at[taker].add(shifted)
    labels = jnp.searchsorted(jnp.cumsum(sizes), jnp.arange(rows * top), side="right").astype(jnp.int32)
    grid = labels.reshape(top, rows).T
    grid = grid[jax.random.permutation(jax.random.fold_in(own, 1), rows)]
    turn = jax.random.randint(jax.random.fold_in(own, 2), (rows, 1), 0, top)
    return jnp.take_along_axis(grid, (jnp.arange(top)[None, :] + turn) % top, axis=1)


def portions_of(count, total, bound, skew, full):
    weights = [(1 << 20) // math.isqrt(rank ** skew) + 1 for rank in range(1, count + 1)]
    largest = bound if full else min(bound, max(-(-total // count), total * weights[0] // sum(weights)))
    least = 1 if total - largest >= count - 1 else 0
    counts, surplus = [largest] + [least] * (count - 1), total - largest - least * (count - 1)
    while surplus > 0:
        free = [i for i in range(1, count) if counts[i] < largest] or [i for i in range(1, count) if counts[i] < bound]
        pool, budget = sum([weights[i] for i in free]), surplus
        for i in free:
            extra = min(bound - counts[i], max(1, budget * weights[i] // pool), surplus)
            counts[i] = counts[i] + extra
            surplus = surplus - extra
    return np.array(counts)


def scatter_about(own_key, shape, width, most, split=(), kind=jnp.bfloat16):
    drawn = jax.random.normal(own_key, shape, jnp.float32) * width
    if len(split) > 0:
        drawn = steps_of(own_key, shape, split, -0.22, 0.18) * drawn
    return jnp.clip(drawn, min=-most, max=most).astype(kind)


def setup_inputs(seed: int = 0) -> dict:
    keys = jax.random.split(jax.random.key(seed), 9)
    grad_out = scatter_about(keys[0], (TOKENS, D), 1.0, 6.0, ((0, 16),))
    parked_inputs = scatter_about(keys[1], (2, TOKENS, HALF), 1.0, 6.0, ((0, 2), (1, 16)))
    route_ids_keys = jax.random.split(jax.random.fold_in(keys[2], 1), TOKENS // TOK)
    route_ids_turns = jax.random.permutation(jax.random.fold_in(keys[2], 3), TOKENS // TOK)
    route_ids = jax.vmap(lambda own, number: shared_out(jax.random.fold_in(keys[2], 2), own, number, TOK, EXPERTS, TOPK, CAP, 1))(route_ids_keys, route_ids_turns).reshape((TOKENS, TOPK))
    route_probs = jnp.clip(0.1 + 0.79999997 * jax.random.uniform(keys[3], (TOKENS, TOPK), jnp.float32) ** steps_of(keys[3], (TOKENS, TOPK), ((0, 16),), -0.2, 0.2), 0.1, 0.9)
    flight_expert = jax.random.randint(keys[4], (1,), 0, EXPERTS).astype(jnp.int32)
    w_gate = scatter_about(keys[5], (D, FF), D ** -0.5, 0.078125, ((1, 16),))
    w_up = scatter_about(keys[6], (D, FF), D ** -0.5, 0.078125, ((1, 16),))
    w_down = scatter_about(keys[7], (FF, D), FF ** -0.5, 0.0625, ((0, 16),))
    return dict(grad_out=grad_out, parked_inputs=parked_inputs, route_ids=route_ids, route_probs=route_probs, flight_expert=flight_expert, w_gate=w_gate, w_up=w_up, w_down=w_down)


def reference(grad_out, parked_inputs, route_ids, route_probs, flight_expert, w_gate, w_up, w_down):
    inputs = jnp.concatenate([parked_inputs[0], parked_inputs[1]], axis=1)
    hits = route_ids == flight_expert[0]
    weight = jnp.sum(jnp.where(hits, route_probs, jnp.float32(0.0)), axis=1)
    flags = jnp.any(hits, axis=1).astype(jnp.int32).reshape(N_EP, TOK)
    ranks = jnp.cumsum(flags, axis=1) - flags
    slot_ids = jnp.arange(CAP, dtype=jnp.int32)
    match = (ranks[:, None, :] == slot_ids[None, :, None]) & (flags[:, None, :] == 1)
    token_ids = jnp.arange(TOK, dtype=jnp.int32)
    slot_tok = jnp.sum(jnp.where(match, token_ids[None, None, :], 0), axis=2).astype(jnp.int32)
    valid = jnp.any(match, axis=2).reshape(-1, 1)
    row_index = (slot_tok + (jnp.arange(N_EP, dtype=jnp.int32) * TOK)[:, None]).reshape(-1)
    zero = jnp.zeros((), jnp.bfloat16)
    rows_x = jnp.where(valid, inputs[row_index], zero)
    rows_dy = jnp.where(valid, grad_out[row_index], zero)
    gate = jnp.dot(rows_x, w_gate, preferred_element_type=jnp.float32)
    up = jnp.dot(rows_x, w_up, preferred_element_type=jnp.float32)
    dhid = jnp.dot(rows_dy, w_down.T, preferred_element_type=jnp.float32)
    sig = jax.nn.sigmoid(gate)
    d_up = (dhid * gate * sig).astype(jnp.bfloat16)
    d_gate = (dhid * up * sig * (1.0 + gate * (1.0 - sig))).astype(jnp.bfloat16)
    rows_dx = jnp.dot(d_gate, w_gate.T, preferred_element_type=jnp.float32) + jnp.dot(d_up, w_up.T, preferred_element_type=jnp.float32)
    contrib = jnp.einsum("bct,bcd->btd", match.astype(jnp.float32), rows_dx.reshape(N_EP, CAP, -1), precision=lax.Precision.HIGHEST)
    contrib = contrib.reshape(N_EP * TOK, -1)
    total = grad_out.astype(jnp.float32) + 0.5 * weight[:, None] * contrib
    return total.astype(jnp.bfloat16)
```

```python
import functools

import jax
import jax.numpy as jnp
from jax import lax
from jax.experimental import pallas as pl
from jax.experimental.pallas import tpu as pltpu
from jax.sharding import PartitionSpec as P

CAP = 34
PIECES = 4
MIN_HIDDEN = 512
GROUPS = ((0, 1, 2, 3),)
f32 = jnp.float32
bf16 = jnp.bfloat16


def flip(value, bit):
    size = lax.axis_size("ep")
    return lax.ppermute(value, "ep", [(s, s ^ (1 << bit)) for s in range(size)])


def ring_next(value, ring):
    size = lax.axis_size("ep")
    span = 4 * ring
    pairs = []
    for s in range(size):
        base, inner = s // span * span, s % span
        pairs.append((s, base + (inner + 4) % span))
    return lax.ppermute(value, "ep", pairs)


def slots_of(fe_ref, ids_ref):
    ids = ids_ref[...]
    hits = (ids == fe_ref[0]).astype(f32)
    flags = jnp.max(hits, axis=1, keepdims=True)
    tokens = ids.shape[0]
    row = lax.broadcasted_iota(jnp.int32, (tokens, tokens), 0)
    col = lax.broadcasted_iota(jnp.int32, (tokens, tokens), 1)
    before = (col < row).astype(bf16)
    ranks = jnp.dot(before, jnp.broadcast_to(flags, (tokens, 128)).astype(bf16), preferred_element_type=f32)
    slot = lax.broadcasted_iota(jnp.int32, (tokens, CAP), 1).astype(f32)
    match = (ranks[:, :1] == slot) & (flags > 0.5)
    return match, hits


def rows_body(core_ref, fe_ref, ids_ref, x_ref, dy_ref, out_ref):
    match, _ = slots_of(fe_ref, ids_ref)
    pick = match.astype(bf16)
    dims = (((0,), (0,)), ((), ()))
    xr = lax.dot_general(pick, x_ref[...], dims, preferred_element_type=f32).astype(bf16)
    dyr = lax.dot_general(pick, dy_ref[...], dims, preferred_element_type=f32).astype(bf16)
    width = out_ref.shape[1]
    parts = []
    for rows in (xr, dyr):
        for q in range(PIECES):
            parts.append(rows[:, q * width:(q + 1) * width])
    out_ref[...] = jnp.concatenate(parts, axis=0)


def build_rows(core, flight_expert, route_ids, own_half, grad_out):
    tokens, half = own_half.shape
    width = half // PIECES
    whole = lambda i, c, f: (0, 0)
    return pl.pallas_call(
        rows_body,
        grid_spec=pltpu.PrefetchScalarGridSpec(
            num_scalar_prefetch=2,
            grid=(1,),
            in_specs=[
                pl.BlockSpec(route_ids.shape, whole),
                pl.BlockSpec((tokens, half), whole),
                pl.BlockSpec((tokens, half), lambda i, c, f: (0, c[0])),
            ],
            out_specs=pl.BlockSpec((2 * PIECES * CAP, width), whole),
        ),
        out_shape=jax.ShapeDtypeStruct((2 * PIECES * CAP, width), bf16),
        name="rows",
    )(core, flight_expert, route_ids, own_half, grad_out)


def first_body(n, core_ref, *refs):
    chunks = refs[:5 * n]
    wg, wu, wd, out, out_low = refs[5 * n:]
    q = pl.program_id(0)
    dy_at = PIECES * CAP

    def part(piece):
        xs, dys = [], []
        low = piece * CAP
        for b in range(n):
            own, fx, fy, dlo, dhi = chunks[5 * b:5 * b + 5]
            for ref in (own, fx, fy, dlo):
                xs.append(ref[low:low + CAP, :])
            for ref in (own, fx, fy):
                dys.append(ref[dy_at + low:dy_at + low + CAP, :])
            dys.append(dhi[low:low + CAP, :])
        x = jnp.concatenate(xs, axis=0)
        dy = jnp.concatenate(dys, axis=0)
        g = jnp.dot(x, wg[...], preferred_element_type=f32)
        u = jnp.dot(x, wu[...], preferred_element_type=f32)
        h = lax.dot_general(dy, wd[...], (((1,), (1,)), ((), ())), preferred_element_type=f32)
        r = jnp.concatenate([g, u, h], axis=1)
        if piece == 0:
            out[...] = r
        else:
            out[...] += r
        if piece == PIECES - 1:
            out_low[...] = out[...].astype(bf16)

    for piece in range(PIECES):
        pl.when(q == piece)(functools.partial(part, piece))


def first(core, blocks, w_gate, w_up, w_down):
    n = len(blocks)
    hidden = w_gate.shape[1]
    width = blocks[0][0].shape[1]
    rows = 4 * n * CAP
    whole = lambda q, c: (0, 0)
    arrays = [a for b in blocks for a in b]
    in_specs = [pl.BlockSpec(a.shape, whole) for a in arrays]
    in_specs += [
        pl.BlockSpec((width, hidden), lambda q, c: (c[0] * PIECES + q, 0)),
        pl.BlockSpec((width, hidden), lambda q, c: (c[0] * PIECES + q, 0)),
        pl.BlockSpec((hidden, width), lambda q, c: (0, c[0] * PIECES + q)),
    ]
    return pl.pallas_call(
        functools.partial(first_body, n),
        grid_spec=pltpu.PrefetchScalarGridSpec(
            num_scalar_prefetch=1,
            grid=(PIECES,),
            in_specs=in_specs,
            out_specs=[pl.BlockSpec((rows, 3 * hidden), whole)] * 2,
        ),
        out_shape=[
            jax.ShapeDtypeStruct((rows, 3 * hidden), f32),
            jax.ShapeDtypeStruct((rows, 3 * hidden), bf16),
        ],
        compiler_params=pltpu.CompilerParams(vmem_limit_bytes=48 << 20),
        name="first",
    )(core, *arrays, w_gate, w_up, w_down)


def second_body(n, core_ref, mine_ref, theirs_ref, wg, wu, *refs):
    outs = refs[:4 * n]
    dg_ref, du_ref = refs[4 * n:]
    q = pl.program_id(0)
    hidden = wg.shape[1]

    @pl.when(q == 0)
    def _():
        total = mine_ref[...] + theirs_ref[...].astype(f32)
        gate = total[:, :hidden]
        up = total[:, hidden:2 * hidden]
        dhid = total[:, 2 * hidden:]
        sig = jax.nn.sigmoid(gate)
        du_ref[...] = (dhid * gate * sig).astype(bf16)
        dg_ref[...] = (dhid * up * sig * (1.0 + gate * (1.0 - sig))).astype(bf16)

    dims = (((1,), (1,)), ((), ()))

    def part(piece):
        r = lax.dot_general(dg_ref[...], wg[...], dims, preferred_element_type=f32)
        r = r + lax.dot_general(du_ref[...], wu[...], dims, preferred_element_type=f32)
        r = r.astype(bf16)
        for i in range(4 * n):
            outs[i][piece * CAP:(piece + 1) * CAP, :] = r[i * CAP:(i + 1) * CAP, :]

    for piece in range(PIECES):
        pl.when(q == piece)(functools.partial(part, piece))


def second(core, n, mine, theirs, w_gate, w_up, width):
    hidden = w_gate.shape[1]
    rows = mine.shape[0]
    whole = lambda q, c: (0, 0)
    outs = pl.pallas_call(
        functools.partial(second_body, n),
        grid_spec=pltpu.PrefetchScalarGridSpec(
            num_scalar_prefetch=1,
            grid=(PIECES,),
            in_specs=[
                pl.BlockSpec(mine.shape, whole),
                pl.BlockSpec(theirs.shape, whole),
                pl.BlockSpec((width, hidden), lambda q, c: (c[0] * PIECES + q, 0)),
                pl.BlockSpec((width, hidden), lambda q, c: (c[0] * PIECES + q, 0)),
            ],
            out_specs=[pl.BlockSpec((PIECES * CAP, width), whole)] * (4 * n),
            scratch_shapes=[pltpu.VMEM((rows, hidden), bf16)] * 2,
        ),
        out_shape=[jax.ShapeDtypeStruct((PIECES * CAP, width), bf16)] * (4 * n),
        compiler_params=pltpu.CompilerParams(vmem_limit_bytes=48 << 20),
        name="second",
    )(core, mine, theirs, w_gate, w_up)
    return [outs[4 * i:4 * i + 4] for i in range(n)]


def last_body(core_ref, fe_ref, ids_ref, probs_ref, grad_ref, p0_ref, sx_ref, sy_ref, sz_ref, out_ref):
    match, hits = slots_of(fe_ref, ids_ref)
    pick = match.astype(bf16)
    weight = jnp.sum(hits * probs_ref[...], axis=1, keepdims=True)
    total = (p0_ref[...].astype(f32) + sx_ref[...].astype(f32)) + (sy_ref[...].astype(f32) + sz_ref[...].astype(f32))
    width = total.shape[1]
    for q in range(PIECES):
        rows = total[q * CAP:(q + 1) * CAP, :]
        high = rows.astype(bf16)
        low = (rows - high.astype(f32)).astype(bf16)
        contrib = jnp.dot(pick, high, preferred_element_type=f32) + jnp.dot(pick, low, preferred_element_type=f32)
        at = slice(q * width, (q + 1) * width)
        out_ref[:, at] = (grad_ref[:, at].astype(f32) + 0.5 * weight * contrib).astype(bf16)


def finish(core, flight_expert, route_ids, route_probs, grad_out, parts):
    tokens = grad_out.shape[0]
    half = grad_out.shape[1] // 2
    whole = lambda i, c, f: (0, 0)
    return pl.pallas_call(
        last_body,
        grid_spec=pltpu.PrefetchScalarGridSpec(
            num_scalar_prefetch=2,
            grid=(1,),
            in_specs=[
                pl.BlockSpec(route_ids.shape, whole),
                pl.BlockSpec(route_probs.shape, whole),
                pl.BlockSpec((tokens, half), lambda i, c, f: (0, c[0])),
            ] + [pl.BlockSpec(p.shape, whole) for p in parts],
            out_specs=pl.BlockSpec((tokens, half), whole),
        ),
        out_shape=jax.ShapeDtypeStruct((tokens, half), bf16),
        name="last",
    )(core, flight_expert, route_ids, route_probs, grad_out, *parts)


def swap_cores(value):
    return lax.ppermute(value, "swap", [(0, 1), (1, 0)])


def on_device(grad_out, parked_inputs, route_ids, route_probs, flight_expert, w_gate, w_up, w_down):
    core = lax.axis_index("swap").reshape(1)
    size = lax.axis_size("ep")
    spread = max(1, MIN_HIDDEN // w_gate.shape[1])
    ring = size // spread // 4
    for bit in range((4 * ring).bit_length() - 1, size.bit_length() - 1):
        w_gate = jnp.concatenate([w_gate, flip(w_gate, bit)], axis=1)
        w_up = jnp.concatenate([w_up, flip(w_up, bit)], axis=1)
        w_down = jnp.concatenate([w_down, flip(w_down, bit)], axis=0)

    own = build_rows(core, flight_expert, route_ids, parked_inputs[0], grad_out)
    mid = own.shape[0] // 2
    blocks = []
    block = own
    for j in range(ring):
        fx = flip(block, 0)
        fy = flip(block, 1)
        onward = ring_next(block, ring) if j + 1 < ring else None
        dlo = flip(fx[:mid], 1)
        dhi = flip(fy[mid:], 0)
        blocks.append((block, fx, fy, dlo, dhi))
        block = onward

    partials = [None] * ring
    width = own.shape[1]
    for group in GROUPS:
        mine, low = first(core, [blocks[j] for j in group], w_gate, w_up, w_down)
        theirs = swap_cores(low)
        outs = second(core, len(group), mine, theirs, w_gate, w_up, width)
        for j, o in zip(group, outs):
            partials[j] = o

    split = mid // 16 * 8
    carry = None
    for j in list(range(1, ring)) + [0]:
        p0, px, py, pd = partials[j]
        ra = flip(pd[:split], 1)
        rb = flip(pd[split:], 0)
        px = jnp.concatenate([px[:split] + ra, px[split:]], axis=0)
        py = jnp.concatenate([py[:split], py[split:] + rb], axis=0)
        sx = flip(px, 0)
        sy = flip(py, 1)
        if j > 0:
            total = p0.astype(f32) + sx.astype(f32) + sy.astype(f32)
            if carry is not None:
                total = total + carry.astype(f32)
            carry = ring_next(total.astype(bf16), ring)
    return finish(core, flight_expert, route_ids, route_probs, grad_out, (p0, sx, sy, carry))


def solution(mesh):
    in_specs = (
        P("ep", None),
        P("swap", "ep", None),
        P("ep", None),
        P("ep", None),
        P(),
        P(None, "ep"),
        P(None, "ep"),
        P("ep", None),
    )
    return jax.shard_map(
        on_device, mesh=mesh, in_specs=in_specs, out_specs=P("ep", "swap"), check_vma=False
    )
```

```python
import functools

import jax
import jax.numpy as jnp
from jax import lax
from jax.experimental import pallas as pl
from jax.experimental.pallas import tpu as pltpu
from jax.sharding import PartitionSpec as P


CAP = 34
PIECES = 4
RING = 4
KERNEL_VMEM = 24 << 20
f32 = jnp.float32
bf16 = jnp.bfloat16


def flip(value, bit):
    size = lax.axis_size("ep")
    return lax.ppermute(value, "ep", [(s, s ^ (1 << bit)) for s in range(size)])


def ring_next(value, ring):
    size = lax.axis_size("ep")
    span = 4 * ring
    pairs = []
    for s in range(size):
        base, inner = s // span * span, s % span
        pairs.append((s, base + (inner + 4) % span))
    return lax.ppermute(value, "ep", pairs)


VMEM_WHOLE = pl.BlockSpec(memory_space=pltpu.VMEM)
SMEM_WHOLE = pl.BlockSpec(memory_space=pltpu.SMEM)
HBM_WHOLE = pl.BlockSpec(memory_space=pltpu.HBM)


def in_hbm(*values):
    return [pltpu.with_memory_space_constraint(value, pltpu.HBM) for value in values]


def slots_of(fe_ref, ids_ref):
    hits = (ids_ref[...] == fe_ref[0]).astype(f32)
    flags = jnp.max(hits, axis=0, keepdims=True)
    tokens = flags.shape[1]
    row = lax.broadcasted_iota(jnp.int32, (tokens, tokens), 0)
    col = lax.broadcasted_iota(jnp.int32, (tokens, tokens), 1)
    before = (row < col).astype(bf16)
    ranks = jnp.dot(jnp.broadcast_to(flags, (16, tokens)).astype(bf16), before, preferred_element_type=f32)
    slot = lax.broadcasted_iota(jnp.int32, (CAP, tokens), 0).astype(f32)
    match = (ranks[:1] == slot) & (flags > 0.5)
    return match.astype(f32).astype(bf16), hits


def rows_body(core_ref, fe_ref, ids_ref, x_hbm, dy_hbm, out_ref, x_ref, dy_ref, sems):
    half = x_ref.shape[1]
    here = pl.ds(pl.multiple_of(core_ref[0] * half, 128), half)
    get_x = pltpu.make_async_copy(x_hbm.at[0], x_ref, sems.at[0])
    get_dy = pltpu.make_async_copy(dy_hbm.at[:, here], dy_ref, sems.at[1])
    get_x.start()
    get_dy.start()
    pick, _ = slots_of(fe_ref, ids_ref)
    width = out_ref.shape[1]
    for i, (copy, ref) in enumerate(((get_x, x_ref), (get_dy, dy_ref))):
        copy.wait()
        rows = jnp.dot(pick, ref[...], preferred_element_type=f32).astype(bf16)
        for q in range(PIECES):
            at = (i * PIECES + q) * CAP
            out_ref[at:at + CAP, :] = rows[:, q * width:(q + 1) * width]


def build_rows(core, flight_expert, ids, parked, grad_out):
    tokens, half = parked.shape[1:]
    width = half // PIECES
    return pl.pallas_call(
        rows_body,
        in_specs=[SMEM_WHOLE, SMEM_WHOLE, VMEM_WHOLE, HBM_WHOLE, HBM_WHOLE],
        out_specs=VMEM_WHOLE,
        out_shape=jax.ShapeDtypeStruct((2 * PIECES * CAP, width), bf16),
        scratch_shapes=[
            pltpu.VMEM((tokens, half), bf16),
            pltpu.VMEM((tokens, half), bf16),
            pltpu.SemaphoreType.DMA((2,)),
        ],
        compiler_params=pltpu.CompilerParams(vmem_limit_bytes=KERNEL_VMEM),
        name="rows",
    )(core, flight_expert, ids, *in_hbm(parked, grad_out))


def prep_body(core_ref, wg, wu, wd, og, ou, od, sems):
    half = og.shape[0]
    here = pl.ds(pl.multiple_of(core_ref[0] * half, 128), half)
    copies = (
        pltpu.make_async_copy(wg.at[here, :], og, sems.at[0]),
        pltpu.make_async_copy(wu.at[here, :], ou, sems.at[1]),
        pltpu.make_async_copy(wd.at[:, here], od, sems.at[2]),
    )
    for copy in copies:
        copy.start()
    for copy in copies:
        copy.wait()


def prep(core, w_gate, w_up, w_down):
    features, hidden = w_gate.shape
    half = features // 2
    return pl.pallas_call(
        prep_body,
        in_specs=[SMEM_WHOLE] + [HBM_WHOLE] * 3,
        out_specs=[VMEM_WHOLE] * 3,
        out_shape=[
            pltpu.VMEM((half, hidden), bf16),
            pltpu.VMEM((half, hidden), bf16),
            pltpu.VMEM((hidden, half), bf16),
        ],
        scratch_shapes=[pltpu.SemaphoreType.DMA((3,))],
        compiler_params=pltpu.CompilerParams(vmem_limit_bytes=KERNEL_VMEM),
        name="prep",
    )(core, *in_hbm(w_gate, w_up, w_down))


def first_body(plan, *refs):
    n = len(refs) - 5
    wg, wu, wd, out, out_low = refs[n:]
    width = refs[0].shape[1]
    total = None
    for q in range(PIECES):
        x = jnp.concatenate([refs[i][at + q * CAP:at + (q + 1) * CAP, :] for (i, at), _ in plan], axis=0)
        dy = jnp.concatenate([refs[i][at + q * CAP:at + (q + 1) * CAP, :] for _, (i, at) in plan], axis=0)
        here = slice(q * width, (q + 1) * width)
        g = jnp.dot(x, wg[here, :], preferred_element_type=f32)
        u = jnp.dot(x, wu[here, :], preferred_element_type=f32)
        h = lax.dot_general(dy, wd[:, here], (((1,), (1,)), ((), ())), preferred_element_type=f32)
        r = jnp.concatenate([g, u, h], axis=1)
        total = r if total is None else total + r
    out[...] = total
    out_low[...] = total.astype(bf16)


def first(arrays, plan, w_gate, w_up, w_down):
    hidden = w_gate.shape[1]
    rows = len(plan) * CAP
    return pl.pallas_call(
        functools.partial(first_body, plan),
        in_specs=[VMEM_WHOLE] * (len(arrays) + 3),
        out_specs=[VMEM_WHOLE] * 2,
        out_shape=[
            jax.ShapeDtypeStruct((rows, 3 * hidden), f32),
            jax.ShapeDtypeStruct((rows, 3 * hidden), bf16),
        ],
        compiler_params=pltpu.CompilerParams(vmem_limit_bytes=KERNEL_VMEM),
        name="first",
    )(*arrays, w_gate, w_up, w_down)


def second_body(mine_ref, theirs_ref, wg, wu, *outs):
    hidden = wg.shape[1]
    width = outs[0].shape[1]
    total = mine_ref[...] + theirs_ref[...].astype(f32)
    gate = total[:, :hidden]
    up = total[:, hidden:2 * hidden]
    dhid = total[:, 2 * hidden:]
    sig = jax.nn.sigmoid(gate)
    du = (dhid * gate * sig).astype(bf16)
    dg = (dhid * up * sig * (1.0 + gate * (1.0 - sig))).astype(bf16)
    dims = (((1,), (1,)), ((), ()))
    for q in range(PIECES):
        here = slice(q * width, (q + 1) * width)
        r = lax.dot_general(dg, wg[here, :], dims, preferred_element_type=f32)
        r = r + lax.dot_general(du, wu[here, :], dims, preferred_element_type=f32)
        r = r.astype(bf16)
        for i, out in enumerate(outs):
            out[q * CAP:(q + 1) * CAP, :] = r[i * CAP:(i + 1) * CAP, :]


def second(mine, theirs, w_gate, w_up, width):
    n = mine.shape[0] // CAP
    return pl.pallas_call(
        second_body,
        in_specs=[VMEM_WHOLE] * 4,
        out_specs=[VMEM_WHOLE] * n,
        out_shape=[jax.ShapeDtypeStruct((PIECES * CAP, width), bf16)] * n,
        compiler_params=pltpu.CompilerParams(vmem_limit_bytes=KERNEL_VMEM),
        name="second",
    )(mine, theirs, w_gate, w_up)


def last_body(core_ref, fe_ref, ids_ref, probs_ref, grad_hbm, p0_ref, sx_ref, sy_ref, sz_ref, out_ref, grad_ref, sem):
    half = grad_ref.shape[1]
    here = pl.ds(pl.multiple_of(core_ref[0] * half, 128), half)
    get = pltpu.make_async_copy(grad_hbm.at[:, here], grad_ref, sem)
    get.start()
    pick, hits = slots_of(fe_ref, ids_ref)
    weight = 0.5 * jnp.sum(hits * probs_ref[...], axis=0, keepdims=True)
    weight = jnp.broadcast_to(weight, (8, weight.shape[1])).T[:, :1]
    total = (p0_ref[...].astype(f32) + sx_ref[...].astype(f32)) + (sy_ref[...].astype(f32) + sz_ref[...].astype(f32))
    high = total.astype(bf16)
    low = (total - high.astype(f32)).astype(bf16)
    width = total.shape[1]
    dims = (((0,), (0,)), ((), ()))
    get.wait()
    for q in range(PIECES):
        at = slice(q * CAP, (q + 1) * CAP)
        contrib = lax.dot_general(pick, high[at], dims, preferred_element_type=f32)
        contrib = contrib + lax.dot_general(pick, low[at], dims, preferred_element_type=f32)
        here = slice(q * width, (q + 1) * width)
        out_ref[:, here] = (grad_ref[:, here].astype(f32) + weight * contrib).astype(bf16)


def finish(core, flight_expert, ids, probs, grad_out, parts):
    tokens = grad_out.shape[0]
    half = grad_out.shape[1] // 2
    return pl.pallas_call(
        last_body,
        in_specs=[SMEM_WHOLE, SMEM_WHOLE, VMEM_WHOLE, VMEM_WHOLE, HBM_WHOLE] + [VMEM_WHOLE] * len(parts),
        out_specs=VMEM_WHOLE,
        out_shape=jax.ShapeDtypeStruct((tokens, half), bf16),
        scratch_shapes=[pltpu.VMEM((tokens, half), bf16), pltpu.SemaphoreType.DMA],
        compiler_params=pltpu.CompilerParams(vmem_limit_bytes=KERNEL_VMEM),
        name="last",
    )(core, flight_expert, ids, probs, *in_hbm(grad_out), *parts)


def swap_cores(value):
    return lax.ppermute(value, "swap", [(0, 1), (1, 0)])


def on_device(grad_out, parked_inputs, route_ids, route_probs, flight_expert, w_gate, w_up, w_down):
    core = lax.axis_index("swap").reshape(1)
    size = lax.axis_size("ep")
    for bit in range((4 * RING).bit_length() - 1, size.bit_length() - 1):
        w_gate = jnp.concatenate([w_gate, flip(w_gate, bit)], axis=1)
        w_up = jnp.concatenate([w_up, flip(w_up, bit)], axis=1)
        w_down = jnp.concatenate([w_down, flip(w_down, bit)], axis=0)

    ids = route_ids.T

    def over_x(value):
        return flip(value, 0)

    def over_y(value):
        return flip(value, 1)

    def over_z(value):
        return ring_next(value, RING)

    own = build_rows(core, flight_expert, ids, parked_inputs, grad_out)
    w_gate, w_up, w_down = prep(core, w_gate, w_up, w_down)
    mid = own.shape[0] // 2
    width = own.shape[1]
    split = mid // 16 * 8

    chunk = [own]
    for _ in range(1, RING):
        chunk.append(over_z(chunk[-1]))
    from_x, parts = [None] * RING, [None] * RING
    for j in range(RING):
        if j == 2:
            fx = over_z(from_x[1])
            fy = over_y(chunk[2])
            arrays = (chunk[2], fx, fy, over_x(fy))
            plan = tuple(((i, 0), (i, mid)) for i in range(4))
        else:
            fx = over_x(chunk[j])
            fy = over_y(chunk[j])
            dl = over_y(fx[:mid])
            dh = over_x(fy[mid:])
            arrays = (chunk[j], fx, fy, dl, dh)
            plan = tuple(((i, 0), (i, mid)) for i in range(3)) + (((3, 0), (4, 0)),)
        from_x[j] = fx
        mine, low = first(arrays, plan, w_gate, w_up, w_down)
        theirs = swap_cores(low)
        parts[j] = second(mine, theirs, w_gate, w_up, width)

    def add(*values):
        total = values[0].astype(f32)
        for value in values[1:]:
            total = total + value.astype(f32)
        return total.astype(bf16)

    def low_rows(piece):
        return jnp.pad(piece.astype(f32), ((0, mid - split), (0, 0)))

    def high_rows(piece):
        return jnp.pad(piece.astype(f32), ((split, 0), (0, 0)))

    p0, px, py, pd = parts[1]
    py = add(py, over_x(pd))
    carry = over_z(add(p0, over_y(py)))
    carry_x = over_z(px)
    for j in list(range(2, RING)) + [0]:
        p0, px, py, pd = parts[j]
        low = over_y(pd[:split])
        px = add(px, low_rows(low), carry_x) if j == 2 else add(px, low_rows(low))
        py = add(py, high_rows(over_x(pd[split:])))
        sx = over_x(px)
        sy = over_y(py)
        if j > 0:
            carry = over_z(add(p0, sx, sy, carry))
    return finish(core, flight_expert, ids, route_probs.T, grad_out, (p0, sx, sy, carry))


def solution(mesh):
    in_specs = (
        P("ep", None),
        P("swap", "ep", None),
        P("ep", None),
        P("ep", None),
        P(),
        P(None, "ep"),
        P(None, "ep"),
        P("ep", None),
    )

    return jax.shard_map(on_device, mesh=mesh, in_specs=in_specs, out_specs=P("ep", "swap"), check_vma=False)
```
